128 devices in a mesh: wide: 16 (over z, x), narrow: 8 (over y, core).
Axes of the slice: x: 4, y: 4, z: 4, core: 2. Of those that a mesh axis runs over, the one named last changes fastest.
Arguments:
- state: float32 [12, 256, 128, 128], P(None, 'wide', 'narrow'), may hold values from -6 to 6
- wind_x: bfloat16 [256, 128, 128], P('wide', 'narrow'), may hold values from -8 to 8
- wind_y: bfloat16 [256, 128, 128], P('wide', 'narrow'), may hold values from -8 to 8
- level_mix: bfloat16 [128, 128], replicated, may hold values from -0.5 to 0.5
- field_mix: float32 [12, 12], replicated, may hold values from -1.75 to 1.75
- block_cost: int32 [32, 8], P('wide', 'narrow'), may hold values from 6 to 24
Outputs:
- new_state: float32 [12, 256, 128, 128], P(None, 'wide', 'narrow')
- tendency: float32 [12, 256, 128, 128], P(None, 'wide', 'narrow')
The draws below stay inside these ranges and needn't reach their ends.
All inputs are finite; a program needn't handle non-finite values.
Results may differ from the reference program's by a relative error of at most 0.0012.
Values sent between devices are 32-bit elements; how exact they have to be, the bound alone decides.
No kernel may reach another device: no remote copies, remote signals or barrier semaphores. Data moves between devices by JAX's collectives and lax.ppermute only.
A program may use at most 64 MiB of HBM per device.

```python
import math
import jax
import jax.numpy as jnp
from jax import lax

NV = 12
LEV = 128
NP = 4
NSUB = 4
MAXC = 24
BR = 8
PY = 16
NXP = 256
NYP = 128
NBX = 32
N_NARROW = 8


def draw_block_cost(key, part):
    center = jax.random.randint(jax.random.fold_in(key, 11), (), 0, NBX)
    row_index = jnp.arange(NBX)[:, None]
    col_index = jnp.arange(N_NARROW)[None, :]
    distance = jnp.abs(row_index - center)
    distance = jnp.minimum(distance, NBX - distance)
    heavy = 8 * distance < NBX
    high_cost = jax.random.randint(jax.random.fold_in(key, 12), (NBX, N_NARROW), 3 * MAXC // 4, MAXC + 1)
    low_cost = jax.random.randint(jax.random.fold_in(key, 13), (NBX, N_NARROW), MAXC // 4, MAXC // 4 + 3)
    result = jnp.where(heavy, high_cost, low_cost)
    result = jnp.where((row_index == center) & (col_index == 0), MAXC, result)
    far_row = (center + NBX // 2) % NBX
    result = jnp.where((row_index == far_row) & (col_index == 0), MAXC // 4, result)
    return result.astype(jnp.int32)


def draw_state(key, part):
    row_frac = jnp.arange(NXP).astype(jnp.float32) / NXP
    noise = jnp.clip(jax.random.normal(jax.random.fold_in(key, 24), (NV, NXP, NYP, LEV), jnp.float32), -4.0, 4.0)
    offset = jnp.clip(0.8 * jax.random.normal(jax.random.fold_in(key, 25), (NV, 1, 1, LEV), jnp.float32), -2.0, 2.0)
    profile = 0.5 + row_frac
    combined = noise + offset * profile[None, :, None, None]
    return jnp.clip(combined, -6.0, 6.0).astype(jnp.float32)


def level_of(rng, shape, pieces, smallest, largest):
    def one(dim, parts):
        steps = jax.random.uniform(jax.random.fold_in(jax.random.fold_in(rng, 6), dim), (parts,), jnp.float32, smallest / len(pieces), largest / len(pieces))
        return jnp.repeat(jnp.exp(steps), shape[dim] // parts).reshape((-1,) + (1,) * (len(shape) - dim - 1))

    factor_of = one(*pieces[0])
    for cut in pieces[1:]:
        factor_of = factor_of * one(*cut)
    return factor_of


def normal_values(stream_key, dims, deviation, reach, cuts=(), held_as=jnp.bfloat16):
    values = deviation * jax.random.normal(stream_key, dims, jnp.float32)
    if cuts:
        values = values * level_of(stream_key, dims, cuts, -0.22, 0.18)
    return jnp.clip(values, -reach, reach).astype(held_as)


def setup_inputs(seed: int = 0) -> dict:
    splits = jax.random.split(jax.random.key(seed), 7)
    return {
        "state": draw_state(jax.random.fold_in(splits[6], 71), 0),
        "wind_x": normal_values(splits[1], (NXP, NYP, LEV), 1.5, 8.0, ((0, 16), (1, 8))),
        "wind_y": normal_values(splits[2], (NXP, NYP, LEV), 1.5, 8.0, ((0, 16), (1, 8))),
        "level_mix": normal_values(splits[3], (LEV, LEV), LEV ** -0.5, 0.5),
        "field_mix": normal_values(splits[4], (NV, NV), NV ** -0.5, 1.75, (), jnp.float32),
        "block_cost": draw_block_cost(jax.random.fold_in(splits[6], 71), 0),
    }


dyn_step = 0.05

def derivative_table():
    inner = 1.0 / math.sqrt(5.0)
    node_list = jnp.array([-1.0, -inner, inner, 1.0], jnp.float32)
    identity = jnp.eye(4, dtype=jnp.float32)
    spacing = node_list[:, None] - node_list[None, :] + identity
    barycentric = 1.0 / jnp.prod(spacing, axis=1)
    off_diag = barycentric[None, :] / barycentric[:, None] / spacing * (1.0 - identity)
    return off_diag - identity * lax.optimization_barrier(jnp.sum(off_diag, axis=1))[:, None]

def micro_turn(current, level_mix, field_mix):
    rounded = current.astype(jnp.bfloat16)
    mixed = jnp.dot(rounded, level_mix, preferred_element_type=jnp.float32)
    coupled = jnp.einsum('vw,wabl->vabl', field_mix, mixed, precision=lax.Precision.HIGHEST)
    return 0.5 * current + 0.5 * jnp.tanh(coupled)

def divergence(field, wind_x, wind_y, derivative):
    fields, rows, columns, levels = field.shape
    flux_x = (wind_x.astype(jnp.float32)[None] * field).reshape(fields, rows // NP, NP, columns, levels)
    flux_y = (wind_y.astype(jnp.float32)[None] * field).reshape(fields, rows, columns // NP, NP, levels)
    along_x = jnp.einsum('ab,vebyl->veayl', derivative, flux_x, precision=lax.Precision.HIGHEST).reshape(field.shape)
    along_y = jnp.einsum('ab,vxebl->vxeal', derivative, flux_y, precision=lax.Precision.HIGHEST).reshape(field.shape)
    return along_x + along_y

def edge_weights(length):
    position = jnp.arange(length) % NP
    right = (position == NP - 1).astype(jnp.float32)
    left = (position == 0).astype(jnp.float32)
    return (right, left)

def average_copies(div):
    right_x, left_x = edge_weights(div.shape[1])
    right_y, left_y = edge_weights(div.shape[2])
    right_x = right_x[None, :, None, None]
    left_x = left_x[None, :, None, None]
    right_y = right_y[None, None, :, None]
    left_y = left_y[None, None, :, None]
    summed = div + right_x * jnp.roll(div, -1, 1) + left_x * jnp.roll(div, 1, 1)
    summed = summed + right_y * jnp.roll(summed, -1, 2) + left_y * jnp.roll(summed, 1, 2)
    return summed / ((1.0 + right_x + left_x) * (1.0 + right_y + left_y))

def reference(state, wind_x, wind_y, level_mix, field_mix, block_cost):
    fields, rows, columns, levels = state.shape
    row_blocks = rows // BR
    blocks = jnp.moveaxis(state.reshape(fields, row_blocks, BR, columns, levels), 1, 0)
    cost_rows = jnp.repeat(block_cost, PY, axis=1)

    def one_row(packed):
        start, costs = packed

        def turn_body(turn, current):
            updated = micro_turn(current, level_mix, field_mix)
            return jnp.where((costs > turn)[None, None, :, None], updated, current)
        return lax.fori_loop(0, MAXC, turn_body, start) - start
    raw = jnp.moveaxis(lax.map(one_row, (blocks, cost_rows)), 0, 1).reshape(state.shape)
    column_mean = lax.optimization_barrier(jnp.sum(raw, axis=(1, 2))) / (rows * columns)
    tendency = raw - column_mean[:, None, None, :]
    derivative = derivative_table()
    current = state
    for substep in range(NSUB):
        div = divergence(current, wind_x, wind_y, derivative)
        current = current + dyn_step * (tendency - average_copies(div))
    return (current, tendency)
```

```python
import functools
import math

import jax
import jax.numpy as jnp
import numpy as np
from jax import lax
from jax.experimental import pallas as pl
from jax.experimental.pallas import tpu as pltpu
from jax.sharding import PartitionSpec as P

NV = 12
NF = NV + 1
LEV = 128
N = 16
NSUB = 4
STEP = 0.05
F32 = jnp.float32
BF16 = jnp.bfloat16
EXTRA = 8


def derivative_numbers():
    nodes = np.array([-1.0, -1.0 / math.sqrt(5.0), 1.0 / math.sqrt(5.0), 1.0])
    spacing = nodes[:, None] - nodes[None, :] + np.eye(4)
    weights = 1.0 / np.prod(spacing, axis=1)
    off = weights[None, :] / weights[:, None] / spacing * (1.0 - np.eye(4))
    return off - np.diag(off.sum(1))


DER = derivative_numbers()
COPIES = np.array([2.0, 1.0, 1.0, 2.0])
DERC = DER / COPIES[:, None]


def vmem():
    return pl.BlockSpec(memory_space=pltpu.VMEM)


def call(body, name, ins, outs, micros, aliases=None, scratch=(), smem=0):
    specs = [pl.BlockSpec(memory_space=pltpu.SMEM)] * smem
    specs += [vmem()] * (len(ins) - smem)
    return pl.pallas_call(
        body,
        out_shape=tuple(jax.ShapeDtypeStruct(s, F32) for s in outs),
        in_specs=specs,
        out_specs=tuple(vmem() for _ in outs),
        scratch_shapes=list(scratch),
        input_output_aliases=aliases or {},
        compiler_params=pltpu.CompilerParams(vmem_limit_bytes=24 << 20),
        cost_estimate=pl.CostEstimate(
            flops=int(micros * 4e6), bytes_accessed=int(micros * 2e6), transcendentals=0
        ),
        name=name,
    )(*ins)


def field_operator(field_mix):
    row = lax.broadcasted_iota(jnp.int32, (96, NV), 0) // 8
    pick = (row == lax.broadcasted_iota(jnp.int32, (96, NV), 1)).astype(F32)
    wide = lax.dot_general(
        pick, field_mix, (((1,), (0,)), ((), ())),
        precision=lax.Precision.HIGHEST, preferred_element_type=F32,
    )
    wide = lax.dot_general(
        wide, pick, (((1,), (1,)), ((), ())),
        precision=lax.Precision.HIGHEST, preferred_element_type=F32,
    )
    left = lax.broadcasted_iota(jnp.int32, (96, 96), 0) % 8
    right = lax.broadcasted_iota(jnp.int32, (96, 96), 1) % 8
    wide = jnp.where(left == right, wide, 0.0)
    high = wide.astype(BF16)
    low = (wide - high.astype(F32)).astype(BF16)
    return high, low


def physics_body(count_ref, state_ref, level_ref, mix_ref, raw_ref, sum_ref, field_w, level_w):
    high, low = field_operator(mix_ref[...])
    field_w[:, :96] = high
    field_w[:, 96:192] = low
    field_w[:, 192:] = high[:, : 8 * EXTRA]
    level_w[...] = jnp.zeros_like(level_w)
    level_w[:LEV, :LEV] = level_ref[...]
    level_w[LEV:, LEV:] = level_ref[...]
    raw_ref[...] = state_ref[...]

    def part(row, half):
        return (slice(None), slice(16 * row + 8 * half, 16 * row + 8 * half + 8), slice(None))

    def turn(rows):
        now = [[raw_ref[part(r, h)].reshape(96, LEV) for h in range(2)] for r in rows]
        packed = [jnp.concatenate([x.astype(BF16) for x in pair], axis=1) for pair in now]
        mixed = jnp.dot(
            jnp.concatenate(packed, axis=0), level_w[...], preferred_element_type=F32
        )
        for i, r in enumerate(rows):
            y = mixed[96 * i : 96 * i + 96]
            y_high = y.astype(BF16)
            y_low = (y[: 8 * EXTRA] - y_high[: 8 * EXTRA].astype(F32)).astype(BF16)
            coupled = jnp.dot(
                field_w[...],
                jnp.concatenate([y_high, y_high, y_low], axis=0),
                preferred_element_type=F32,
            )
            for h in range(2):
                value = jnp.tanh(coupled[:, LEV * h : LEV * h + LEV])
                raw_ref[part(r, h)] = (0.5 * (now[i][h] + value)).reshape(NV, 8, LEV)

    first = count_ref[0, 0]
    second = count_ref[1, 0]
    both = jnp.minimum(first, second)

    def joint(i, carry):
        turn(range(16))
        return carry

    lax.fori_loop(0, both, joint, 0)
    for block, count in ((0, first), (1, second)):

        def single(i, carry, block=block):
            turn(range(8 * block, 8 * block + 8))
            return carry

        lax.fori_loop(both, count, single, 0)

    def finish(v, carry):
        raw = raw_ref[v] - state_ref[v]
        raw_ref[v] = raw
        sum_ref[pl.ds(v, 1), :] = jnp.sum(raw, axis=0, keepdims=True)
        return carry

    lax.fori_loop(0, NV, finish, 0, unroll=4)


def column_table(shift):
    b = lax.broadcasted_iota(jnp.int32, (8, LEV), 0) % 4
    out = jnp.full((8, LEV), float(DERC[3, 3 ^ shift]), F32)
    for k in range(3):
        out = jnp.where(b == k, float(DERC[k, k ^ shift]), out)
    return out


def tables():
    return [column_table(s) for s in range(4)]


def permuted(x, index):
    return jnp.take_along_axis(x, index, axis=0)


def indices():
    q = lax.broadcasted_iota(jnp.int32, (8, LEV), 0)
    return [q ^ s for s in range(4)]


def along_sublanes(x, coef, index):
    out = coef[0] * x
    for s in range(1, 4):
        out = out + coef[s] * permuted(x, index[s])
    return out


def column_edges(s_ref, v, edge_ref, side, half, coef, index):
    q0 = 0 if side == 0 else 12
    edge = 0 if side == 0 else 3
    rows = []
    for j in range(4):
        rows.append(s_ref[v, pl.ds(128 * half + q0 + j, 8, stride=16), :])
    out = along_sublanes(edge_ref[side, 4, pl.ds(8 * half, 8), :] * rows[edge], coef, index)
    for j in range(4):
        out = out + edge_ref[side, j, pl.ds(8 * half, 8), :] * rows[j]
    return out


def write_edges(fields, s_ref, edge_ref, left_ref, right_ref):
    coef, index = tables(), indices()

    def one(v, carry):
        for side, ref in ((0, left_ref), (1, right_ref)):
            for half in range(2):
                ref[v, pl.ds(8 * half, 8), :] = column_edges(
                    s_ref, v, edge_ref, side, half, coef, index
                )
        return carry

    lax.fori_loop(0, fields, one, 0)


def first_body(s_ref, wx_ref, wy_ref, wxs_ref, wys_ref, edge_ref, left_ref, right_ref):
    q = lax.broadcasted_iota(jnp.int32, (16, LEV), 0) % 4
    inner = (q == 1) | (q == 2)
    per_q = jnp.where(inner, -STEP, -0.5 * STEP)
    for p in range(N):
        rows = pl.ds(16 * p, 16)
        wxs_ref[rows, :] = per_q * wx_ref[rows, :].astype(F32)
        wys_ref[rows, :] = float(-STEP / COPIES[p % 4]) * wy_ref[rows, :].astype(F32)
    for side in range(2):
        q0, edge = (0, 0) if side == 0 else (12, 3)
        for half in range(2):
            at = pl.ds(8 * half, 8)
            for j in range(4):
                wind = wys_ref[pl.ds(128 * half + q0 + j, 8, stride=16), :]
                edge_ref[side, j, at, :] = float(DERC[edge, j]) * wind
            edge_ref[side, 4, at, :] = wxs_ref[pl.ds(128 * half + q0 + edge, 8, stride=16), :]
    write_edges(NV, s_ref, edge_ref, left_ref, right_ref)


def along_rows(f):
    c = DERC
    plus, minus = f[0] + f[3], f[0] - f[3]
    inner_plus, inner_minus = f[1] + f[2], f[1] - f[2]
    even = plus - inner_plus
    a = float(0.5 * (c[0, 0] - c[0, 3])) * minus + float(0.5 * (c[0, 1] - c[0, 2])) * inner_minus
    b = float(0.5 * (c[0, 0] + c[0, 3])) * even
    d = float(0.5 * (c[1, 0] - c[1, 3])) * minus + float(0.5 * (c[1, 1] - c[1, 2])) * inner_minus
    e = float(0.5 * (c[1, 0] + c[1, 3])) * even
    return [a + b, d + e, d - e, a - b]


def full_body(fields, s_ref, wxs_ref, wys_ref, g_ref):
    coef, index = tables(), indices()
    q = lax.broadcasted_iota(jnp.int32, (8, LEV), 0)
    middle = (q == 3) | (q == 4)
    low, high = q == 0, q == 7
    swap = jnp.where(low, 7, jnp.where(high, 0, jnp.where(middle, 7 - q, q)))

    def one(v, carry):
        for e in range(4):
            halves = []
            for half in range(2):
                at = [pl.ds(64 * e + 16 * a + 8 * half, 8) for a in range(4)]
                s = [s_ref[v, at[a], :] for a in range(4)]
                x = along_rows([wxs_ref[at[a], :] * s[a] for a in range(4)])
                halves.append(
                    [
                        x[a] + along_sublanes(wys_ref[at[a], :] * s[a], coef, index)
                        for a in range(4)
                    ]
                )
            for a in range(4):
                left, right = halves[0][a], halves[1][a]
                p_left, p_right = permuted(left, swap), permuted(right, swap)
                left = left + jnp.where(high, p_right, jnp.where(middle, p_left, 0.0))
                right = right + jnp.where(low, p_left, jnp.where(middle, p_right, 0.0))
                g_ref[v, pl.ds(64 * e + 16 * a, 8), :] = left
                g_ref[v, pl.ds(64 * e + 16 * a + 8, 8), :] = right
        return carry

    lax.fori_loop(0, fields, one, 0)


def with_columns(g_ref, from_left, from_right, v, p, low, high):
    left = g_ref[v, pl.ds(16 * p, 8), :]
    right = g_ref[v, pl.ds(16 * p + 8, 8), :]
    left = left + jnp.where(low, from_left[v, pl.ds(p, 1), :], 0.0)
    right = right + jnp.where(high, from_right[v, pl.ds(p, 1), :], 0.0)
    return left, right


def ends():
    q = lax.broadcasted_iota(jnp.int32, (8, LEV), 0)
    return q == 0, q == 7


def rows_body(fields, summed, g_ref, from_left, from_right, *refs):
    low, high = ends()
    if summed:
        sum_ref, more_ref, top_ref, bottom_ref, total_ref = refs
        total_ref[...] = sum_ref[...] + more_ref[...]
    else:
        top_ref, bottom_ref = refs

    def one(v, carry):
        for p, ref in ((0, top_ref), (N - 1, bottom_ref)):
            left, right = with_columns(g_ref, from_left, from_right, v, p, low, high)
            ref[v, 0:8, :] = left
            ref[v, 8:16, :] = right
        return carry

    lax.fori_loop(0, fields, one, 0)


def advance(s_ref, g_ref, from_left, from_right, v, low, high, source, out_ref):
    g = [with_columns(g_ref, from_left, from_right, v, p, low, high) for p in range(N)]
    for p in range(N):
        mate = p + 1 if p % 4 == 3 else p - 1 if p % 4 == 0 else -1
        for half in range(2):
            at = pl.ds(16 * p + 8 * half, 8)
            value = g[p][half]
            if 0 <= mate < N:
                value = value + g[mate][half]
            value = s_ref[v, at, :] + value
            if source is not None:
                value = value + source(at)
            out_ref[v, at, :] = value


def start_body(s_ref, g_ref, from_left, from_right, out_ref):
    low, high = ends()

    def one(v, carry):
        advance(s_ref, g_ref, from_left, from_right, v, low, high, None, out_ref)
        return carry

    lax.fori_loop(0, NV, one, 0)


def update_body(s_ref, g_ref, from_left, from_right, raw_ref, out_ref):
    low, high = ends()

    def one(v, carry):
        advance(
            s_ref, g_ref, from_left, from_right, v, low, high,
            lambda at: STEP * raw_ref[v, at, :], out_ref,
        )
        return carry

    lax.fori_loop(0, NV, one, 0)
    advance(s_ref, g_ref, from_left, from_right, NV, low, high, lambda at: STEP, out_ref)


def joined_body(s_ref, raw_ref, above_ref, below_ref, edge_ref, out_ref, left_ref, right_ref):
    def one(v, carry):
        out_ref[v] = s_ref[v] + STEP * raw_ref[v]
        out_ref[v, 0:16, :] += above_ref[v]
        out_ref[v, 240:256, :] += below_ref[v]
        return carry

    lax.fori_loop(0, NV, one, 0)
    out_ref[NV] = jnp.full((256, LEV), STEP, F32)
    write_edges(NF, out_ref, edge_ref, left_ref, right_ref)


def edges_body(
    s_ref, above_ref, below_ref, edge_ref, sum_ref, more_ref,
    out_ref, left_ref, right_ref, total_ref,
):
    total_ref[...] = sum_ref[...] + more_ref[...]

    def one(v, carry):
        out_ref[v, 0:16, :] = s_ref[v, 0:16, :] + above_ref[v]
        out_ref[v, 16:240, :] = s_ref[v, 16:240, :]
        out_ref[v, 240:256, :] = s_ref[v, 240:256, :] + below_ref[v]
        return carry

    lax.fori_loop(0, NF, one, 0)
    write_edges(NF, out_ref, edge_ref, left_ref, right_ref)


def last_body(columns, s_ref, r_ref, above_ref, below_ref, r_above, r_below, raw_ref, sum_ref, more_ref,
              new_ref, tend_ref):
    v = pl.program_id(0)
    mean = (sum_ref[pl.ds(v, 1), :] + more_ref[pl.ds(v, 1), :]) * (1.0 / columns)
    tend_ref[0] = raw_ref[0] - mean
    new_ref[0, 16:240, :] = s_ref[0, 16:240, :] - mean * r_ref[0, 16:240, :]
    new_ref[0, 0:16, :] = s_ref[0, 0:16, :] + above_ref[0] - mean * (r_ref[0, 0:16, :] + r_above[0])
    new_ref[0, 240:256, :] = (
        s_ref[0, 240:256, :] + below_ref[0] - mean * (r_ref[0, 240:256, :] + r_below[0])
    )


def last(columns, s, above, below, raw, total, more):
    def field(rows):
        return pl.BlockSpec((1, rows, LEV), lambda v: (v, 0, 0))

    def response(rows):
        return pl.BlockSpec((1, rows, LEV), lambda v: (NV, 0, 0))

    def whole():
        return pl.BlockSpec((NV, LEV), lambda v: (0, 0))

    return pl.pallas_call(
        functools.partial(last_body, columns),
        grid=(NV,),
        out_shape=(jax.ShapeDtypeStruct((NV, 256, LEV), F32),) * 2,
        in_specs=[
            field(256), response(256), field(16), field(16), response(16), response(16),
            field(256), whole(), whole(),
        ],
        out_specs=(field(256), field(256)),
        compiler_params=pltpu.CompilerParams(vmem_limit_bytes=16 << 20),
        cost_estimate=pl.CostEstimate(flops=10**7, bytes_accessed=8 * 10**6, transcendentals=0),
        name="last",
    )(s, s, above, below, above, below, raw, total, more)


def shifted(value, axis, by):
    count = lax.axis_size(axis)
    return lax.ppermute(value, axis, [(i, (i + by) % count) for i in range(count)])


def partner(value, axis, bit):
    count = lax.axis_size(axis)
    return lax.ppermute(value, axis, [(i, i ^ bit) for i in range(count)])


def columns_exchanged(left, right):
    return shifted(right, "narrow", 1), shifted(left, "narrow", -1)


def rows_exchanged(top, bottom):
    return shifted(bottom, "wide", 1), shifted(top, "wide", -1)


def per_device(state, wind_x, wind_y, level_mix, field_mix, block_cost):
    state = state.reshape(NV, 256, LEV)
    wind_x = wind_x.reshape(256, LEV)
    wind_y = wind_y.reshape(256, LEV)
    slab = (256, LEV)
    edge12, edge13 = (NV, N, LEV), (NF, N, LEV)
    wxs, wys, edge, left, right = call(
        first_body, "first", (state, wind_x, wind_y),
        (slab, slab, (2, 5, N, LEV), edge12, edge12), 1,
    )
    from_left, from_right = columns_exchanged(left, right)
    (g,) = call(
        functools.partial(full_body, NV), "full0", (state, wxs, wys), ((NV, 256, LEV),), 3
    )
    top, bottom = call(
        functools.partial(rows_body, NV, False), "rows0", (g, from_left, from_right),
        (edge12, edge12), 0.3,
    )
    above, below = rows_exchanged(top, bottom)
    (moved,) = call(
        start_body, "start", (state, g, from_left, from_right), ((NV, 256, LEV),), 1
    )
    raw, total = call(
        physics_body, "physics", (block_cost, state, level_mix, field_mix),
        ((NV, 256, LEV), (NV, LEV)), 20,
        scratch=(pltpu.VMEM((96, 256), BF16), pltpu.VMEM((256, 256), BF16)), smem=1,
    )
    more = partner(total, "narrow", 1)
    s, left, right = call(
        joined_body, "joined", (moved, raw, above, below, edge),
        ((NF, 256, LEV), edge13, edge13), 1,
    )
    total = total + more
    stages = [("narrow", 2), ("narrow", 4), ("wide", 1), ("wide", 2), ("wide", 4), ("wide", 8)]
    for k in range(1, NSUB):
        from_left, from_right = columns_exchanged(left, right)
        more = partner(total, *stages[2 * k - 2])
        (g,) = call(
            functools.partial(full_body, NF), f"full{k}", (s, wxs, wys), ((NF, 256, LEV),), 3
        )
        top, bottom, total = call(
            functools.partial(rows_body, NF, True), f"rows{k}",
            (g, from_left, from_right, total, more), (edge13, edge13, (NV, LEV)), 0.3,
        )
        above, below = rows_exchanged(top, bottom)
        more = partner(total, *stages[2 * k - 1])
        (s,) = call(
            update_body, f"update{k}", (s, g, from_left, from_right, raw), ((NF, 256, LEV),), 1
        )
        if k < NSUB - 1:
            s, left, right, total = call(
                edges_body, f"edges{k}", (s, above, below, edge, total, more),
                ((NF, 256, LEV), edge13, edge13, (NV, LEV)), 0.7,
            )
    count = 256 * lax.axis_size("wide") * lax.axis_size("narrow")
    new_state, tendency = last(count, s, above, below, raw, total, more)
    return new_state.reshape(NV, N, N, LEV), tendency.reshape(NV, N, N, LEV)


def solution(mesh):
    placed = (
        P(None, "wide", "narrow", None),
        P("wide", "narrow", None),
        P("wide", "narrow", None),
        P(),
        P(),
        P("wide", "narrow"),
    )
    return jax.shard_map(
        per_device,
        mesh=mesh,
        in_specs=placed,
        out_specs=(P(None, "wide", "narrow", None), P(None, "wide", "narrow", None)),
        check_vma=False,
    )
```

```python
import functools
import math

import jax
import jax.numpy as jnp
import numpy as np
from jax import lax
from jax.experimental import pallas as pl
from jax.experimental.pallas import tpu as pltpu
from jax.sharding import PartitionSpec as P


NV = 12
NF = NV + 1
LEV = 128
N = 16
NSUB = 4
STEP = 0.05
F32 = jnp.float32
BF16 = jnp.bfloat16
EXTRA = 8


def derivative_numbers():
    nodes = np.array([-1.0, -1.0 / math.sqrt(5.0), 1.0 / math.sqrt(5.0), 1.0])
    spacing = nodes[:, None] - nodes[None, :] + np.eye(4)
    weights = 1.0 / np.prod(spacing, axis=1)
    off = weights[None, :] / weights[:, None] / spacing * (1.0 - np.eye(4))
    return off - np.diag(off.sum(1))


DER = derivative_numbers()
COPIES = np.array([2.0, 1.0, 1.0, 2.0])
DERC = DER / COPIES[:, None]


def vmem():
    return pl.BlockSpec(memory_space=pltpu.VMEM)


def call(body, ins, outs, micros, aliases=None, scratch=(), smem=0, hbm=0):
    specs = [pl.BlockSpec(memory_space=pltpu.SMEM)] * smem
    specs += [pl.BlockSpec(memory_space=pltpu.HBM)] * hbm
    specs += [vmem()] * (len(ins) - smem - hbm)
    return pl.pallas_call(
      body,
      out_shape=tuple(jax.ShapeDtypeStruct(s, F32) for s in outs),
      in_specs=specs,
      out_specs=tuple(vmem() for _ in outs),
      scratch_shapes=list(scratch),
      input_output_aliases=aliases or {},
      compiler_params=pltpu.CompilerParams(vmem_limit_bytes=6 << 20),
      cost_estimate=pl.CostEstimate(
          flops=int(micros * 4e6), bytes_accessed=int(micros * 2e6), transcendentals=0
      ),
    )(*ins)


def field_operator(field_mix):
    row = lax.broadcasted_iota(jnp.int32, (96, NV), 0) // 8
    pick = (row == lax.broadcasted_iota(jnp.int32, (96, NV), 1)).astype(F32)
    wide = lax.dot_general(
        pick, field_mix, (((1,), (0,)), ((), ())),
        precision=lax.Precision.HIGHEST, preferred_element_type=F32,
    )
    wide = lax.dot_general(
        wide, pick, (((1,), (1,)), ((), ())),
        precision=lax.Precision.HIGHEST, preferred_element_type=F32,
    )
    left = lax.broadcasted_iota(jnp.int32, (96, 96), 0) % 8
    right = lax.broadcasted_iota(jnp.int32, (96, 96), 1) % 8
    wide = jnp.where(left == right, wide, 0.0)
    high = wide.astype(BF16)
    low = (wide - high.astype(F32)).astype(BF16)
    return high, low


def physics_body(
    count_ref, state_ref, level_ref, mix_ref, moved_ref,
    raw_ref, sum_ref, s_ref, field_w, level_w,
):
    high, low = field_operator(mix_ref[...])
    field_w[:, :96] = high
    field_w[:, 96:192] = low
    field_w[:, 192:] = high[:, : 8 * EXTRA]
    level_w[...] = jnp.zeros_like(level_w)
    level_w[:LEV, :LEV] = level_ref[...]
    level_w[LEV:, LEV:] = level_ref[...]
    raw_ref[...] = state_ref[...]

    def part(row, half):
        return (slice(None), slice(16 * row + 8 * half, 16 * row + 8 * half + 8), slice(None))

    def turn(rows):
        now = [[raw_ref[part(r, h)].reshape(96, LEV) for h in range(2)] for r in rows]
        packed = [jnp.concatenate([x.astype(BF16) for x in pair], axis=1) for pair in now]
        mixed = jnp.dot(
            jnp.concatenate(packed, axis=0), level_w[...], preferred_element_type=F32
        )
        for i, r in enumerate(rows):
            y = mixed[96 * i : 96 * i + 96]
            y_high = y.astype(BF16)
            y_low = (y[: 8 * EXTRA] - y_high[: 8 * EXTRA].astype(F32)).astype(BF16)
            coupled = jnp.dot(
                field_w[...],
                jnp.concatenate([y_high, y_high, y_low], axis=0),
                preferred_element_type=F32,
            )
            for h in range(2):
                value = jnp.tanh(coupled[:, LEV * h : LEV * h + LEV])
                raw_ref[part(r, h)] = (0.5 * (now[i][h] + value)).reshape(NV, 8, LEV)

    first = count_ref[0, 0]
    second = count_ref[1, 0]
    both = jnp.minimum(first, second)

    def joint(i, carry):
        turn(range(16))
        return carry

    lax.fori_loop(0, both, joint, 0)
    for block, count in ((0, first), (1, second)):

        def single(i, carry, block=block):
            turn(range(8 * block, 8 * block + 8))
            return carry

        lax.fori_loop(both, count, single, 0)

    def finish(v, carry):
        raw = raw_ref[v] - state_ref[v]
        raw_ref[v] = raw
        s_ref[v] = moved_ref[v] + STEP * raw
        sum_ref[pl.ds(v, 1), :] = jnp.sum(raw, axis=0, keepdims=True)
        return carry

    lax.fori_loop(0, NV, finish, 0, unroll=2)
    s_ref[NV] = jnp.full((256, LEV), STEP, F32)


def column_table(shift):
    b = lax.broadcasted_iota(jnp.int32, (8, LEV), 0) % 4
    out = jnp.full((8, LEV), float(DERC[3, 3 ^ shift]), F32)
    for k in range(3):
        out = jnp.where(b == k, float(DERC[k, k ^ shift]), out)
    return out


def tables():
    return [column_table(s) for s in range(4)]


def permuted(x, index):
    return jnp.take_along_axis(x, index, axis=0)


def indices():
    q = lax.broadcasted_iota(jnp.int32, (8, LEV), 0)
    return [q ^ s for s in range(4)]


def along_sublanes(x, coef, index):
    out = coef[0] * x
    for s in range(1, 4):
        out = out + coef[s] * permuted(x, index[s])
    return out


def column_edges(s_ref, v, edge_ref, side, half, coef, index):
    q0 = 0 if side == 0 else 12
    edge = 0 if side == 0 else 3
    rows = []
    for j in range(4):
        rows.append(s_ref[v, pl.ds(128 * half + q0 + j, 8, stride=16), :])
    out = along_sublanes(edge_ref[side, 4, pl.ds(8 * half, 8), :] * rows[edge], coef, index)
    for j in range(4):
        out = out + edge_ref[side, j, pl.ds(8 * half, 8), :] * rows[j]
    return out


def write_edges(fields, s_ref, edge_ref, left_ref, right_ref):
    coef, index = tables(), indices()

    def one(v, carry):
        for side, ref in ((0, left_ref), (1, right_ref)):
            for half in range(2):
                ref[v, pl.ds(8 * half, 8), :] = column_edges(
                    s_ref, v, edge_ref, side, half, coef, index
                )
        return carry

    lax.fori_loop(0, fields, one, 0)


def first_body(
    state_hbm, wx_hbm, wy_hbm, s_ref, wxs_ref, wys_ref, edge_ref, left_ref, right_ref,
    wx_ref, wy_ref, sems,
):
    winds = [
        pltpu.make_async_copy(wx_hbm, wx_ref, sems.at[NV]),
        pltpu.make_async_copy(wy_hbm, wy_ref, sems.at[NV + 1]),
    ]
    fields = [
        pltpu.make_async_copy(state_hbm.at[v], s_ref.at[v], sems.at[v]) for v in range(NV)
    ]
    for copy in winds + fields:
        copy.start()
    for copy in winds:
        copy.wait()
    q = lax.broadcasted_iota(jnp.int32, (16, LEV), 0) % 4
    inner = (q == 1) | (q == 2)
    per_q = jnp.where(inner, -STEP, -0.5 * STEP)
    for p in range(N):
        rows = pl.ds(16 * p, 16)
        wxs_ref[rows, :] = per_q * wx_ref[rows, :].astype(F32)
        wys_ref[rows, :] = float(-STEP / COPIES[p % 4]) * wy_ref[rows, :].astype(F32)
    for side in range(2):
        q0, edge = (0, 0) if side == 0 else (12, 3)
        for half in range(2):
            at = pl.ds(8 * half, 8)
            for j in range(4):
                wind = wys_ref[pl.ds(128 * half + q0 + j, 8, stride=16), :]
                edge_ref[side, j, at, :] = float(DERC[edge, j]) * wind
            edge_ref[side, 4, at, :] = wxs_ref[pl.ds(128 * half + q0 + edge, 8, stride=16), :]
    for copy in fields:
        copy.wait()
    write_edges(NV, s_ref, edge_ref, left_ref, right_ref)


def along_rows(f):
    c = DERC
    plus, minus = f[0] + f[3], f[0] - f[3]
    inner_plus, inner_minus = f[1] + f[2], f[1] - f[2]
    even = plus - inner_plus
    a = float(0.5 * (c[0, 0] - c[0, 3])) * minus + float(0.5 * (c[0, 1] - c[0, 2])) * inner_minus
    b = float(0.5 * (c[0, 0] + c[0, 3])) * even
    d = float(0.5 * (c[1, 0] - c[1, 3])) * minus + float(0.5 * (c[1, 1] - c[1, 2])) * inner_minus
    e = float(0.5 * (c[1, 0] + c[1, 3])) * even
    return [a + b, d + e, d - e, a - b]


def full_body(fields, s_ref, wxs_ref, wys_ref, *refs):
    if len(refs) == 3:
        refs[2][...] = refs[0][...]
    g_ref = refs[len(refs) // 2]
    coef, index = tables(), indices()
    q = lax.broadcasted_iota(jnp.int32, (8, LEV), 0)
    middle = (q == 3) | (q == 4)
    low, high = q == 0, q == 7
    swap = jnp.where(low, 7, jnp.where(high, 0, jnp.where(middle, 7 - q, q)))

    def one(v, carry):
        for e in range(4):
            halves = []
            for half in range(2):
                at = [pl.ds(64 * e + 16 * a + 8 * half, 8) for a in range(4)]
                s = [s_ref[v, at[a], :] for a in range(4)]
                x = along_rows([wxs_ref[at[a], :] * s[a] for a in range(4)])
                halves.append(
                    [
                        x[a] + along_sublanes(wys_ref[at[a], :] * s[a], coef, index)
                        for a in range(4)
                    ]
                )
            for a in range(4):
                left, right = halves[0][a], halves[1][a]
                p_left, p_right = permuted(left, swap), permuted(right, swap)
                left = left + jnp.where(high, p_right, jnp.where(middle, p_left, 0.0))
                right = right + jnp.where(low, p_left, jnp.where(middle, p_right, 0.0))
                g_ref[v, pl.ds(64 * e + 16 * a, 8), :] = left
                g_ref[v, pl.ds(64 * e + 16 * a + 8, 8), :] = right
        return carry

    lax.fori_loop(0, fields, one, 0)


def with_columns(g_ref, from_left, from_right, v, p, low, high):
    left = g_ref[v, pl.ds(16 * p, 8), :]
    right = g_ref[v, pl.ds(16 * p + 8, 8), :]
    left = left + jnp.where(low, from_left[v, pl.ds(p, 1), :], 0.0)
    right = right + jnp.where(high, from_right[v, pl.ds(p, 1), :], 0.0)
    return left, right


def ends():
    q = lax.broadcasted_iota(jnp.int32, (8, LEV), 0)
    return q == 0, q == 7


def rows_body(fields, g_ref, from_left, from_right, top_ref, bottom_ref):
    low, high = ends()

    def one(v, carry):
        for p, ref in ((0, top_ref), (N - 1, bottom_ref)):
            left, right = with_columns(g_ref, from_left, from_right, v, p, low, high)
            ref[v, 0:8, :] = left
            ref[v, 8:16, :] = right
        return carry

    lax.fori_loop(0, fields, one, 0)


def advance(s_ref, g_ref, from_left, from_right, v, low, high, source, out_ref, inner=False):
    g = [with_columns(g_ref, from_left, from_right, v, p, low, high) for p in range(N)]
    for p in range(N):
        mate = p + 1 if p % 4 == 3 else p - 1 if p % 4 == 0 else -1
        for half in range(2):
            at = pl.ds(16 * p + 8 * half, 8)
            value = g[p][half]
            if 0 <= mate < N:
                value = value + g[mate][half]
            value = s_ref[v, at, :] + value
            if source is not None:
                value = value + source(at)
            if inner:
                out_ref[at, :] = value
            else:
                out_ref[v, at, :] = value


def start_body(s_ref, g_ref, from_left, from_right, top_ref, bottom_ref, out_ref):
    rows_body(NV, g_ref, from_left, from_right, top_ref, bottom_ref)
    low, high = ends()

    def one(v, carry):
        advance(s_ref, g_ref, from_left, from_right, v, low, high, None, out_ref)
        return carry

    lax.fori_loop(0, NV, one, 0)


def update_body(
    s_ref, g_ref, from_left, from_right, raw_ref, sum_ref, out_ref, pass_ref
):
    pass_ref[...] = sum_ref[...]
    low, high = ends()

    def one(v, carry):
        advance(
            s_ref, g_ref, from_left, from_right, v, low, high,
            lambda at: STEP * raw_ref[v, at, :], out_ref,
        )
        return carry

    lax.fori_loop(0, NV, one, 0)
    advance(s_ref, g_ref, from_left, from_right, NV, low, high, lambda at: STEP, out_ref)


def edges_body(s_ref, above_ref, below_ref, edge_ref, out_ref, left_ref, right_ref):
    def one(v, carry):
        out_ref[v, 0:16, :] = s_ref[v, 0:16, :] + above_ref[v]
        out_ref[v, 16:240, :] = s_ref[v, 16:240, :]
        out_ref[v, 240:256, :] = s_ref[v, 240:256, :] + below_ref[v]
        return carry

    lax.fori_loop(0, NV, one, 0)
    if above_ref.shape[0] == NF:
        one(NV, 0)
    else:
        out_ref[NV] = s_ref[NV]
    write_edges(NF, out_ref, edge_ref, left_ref, right_ref)


def output_body(
    columns, s_ref, g_ref, from_left, from_right, raw_ref, sum_ref, more_ref,
    new_hbm, tend_hbm, top_ref, bottom_ref, new_ref, tend_ref, response, sems,
):
    low, high = ends()
    copies = []
    for v in range(NV):
        copies.append(pltpu.make_async_copy(tend_ref.at[v], tend_hbm.at[v], sems.at[0, v]))
        copies.append(pltpu.make_async_copy(new_ref.at[v], new_hbm.at[v], sems.at[1, v]))
    advance(s_ref, g_ref, from_left, from_right, NV, low, high, lambda at: STEP, response, True)
    for v in range(NV):
        mean = (sum_ref[v : v + 1, :] + more_ref[v : v + 1, :]) * (1.0 / columns)
        tend_ref[v] = raw_ref[v] - mean
        copies[2 * v].start()
    for v in range(NV):
        mean = (sum_ref[v : v + 1, :] + more_ref[v : v + 1, :]) * (1.0 / columns)
        advance(
            s_ref, g_ref, from_left, from_right, v, low, high,
            lambda at: STEP * raw_ref[v, at, :] - mean * response[at, :], new_ref.at[v], True,
        )
        copies[2 * v + 1].start()
        top_ref[v] = new_ref[v, 0:16, :]
        bottom_ref[v] = new_ref[v, 240:256, :]
    for copy in copies:
        copy.wait()


def output(columns, s, g, from_left, from_right, raw, total, more):
    anywhere = pl.BlockSpec(memory_space=pltpu.HBM)
    return pl.pallas_call(
      functools.partial(output_body, columns),
      out_shape=(jax.ShapeDtypeStruct((NV, 256, LEV), F32),) * 2
      + (jax.ShapeDtypeStruct((NV, N, LEV), F32),) * 2,
      in_specs=[vmem()] * 7,
      out_specs=(anywhere, anywhere, vmem(), vmem()),
      scratch_shapes=[
          pltpu.VMEM((NV, 256, LEV), F32), pltpu.VMEM((NV, 256, LEV), F32),
          pltpu.VMEM((256, LEV), F32), pltpu.SemaphoreType.DMA((2, NV)),
      ],
      compiler_params=pltpu.CompilerParams(vmem_limit_bytes=8 << 20),
      cost_estimate=pl.CostEstimate(flops=10**7, bytes_accessed=8 * 10**6, transcendentals=0),
      name="output",
    )(s, g, from_left, from_right, raw, total, more)


def patch_body(
    columns, part_ref, top_ref, bottom_ref, above_ref, below_ref, sum_ref, more_ref,
    new_ref, rows_ref, sems,
):
    for v in range(NV):
        mean = (sum_ref[pl.ds(v, 1), :] + more_ref[pl.ds(v, 1), :]) * (1.0 / columns)
        rows_ref[0, v] = top_ref[v] + above_ref[v] - mean * above_ref[NV]
        rows_ref[1, v] = bottom_ref[v] + below_ref[v] - mean * below_ref[NV]
    copies = [
        pltpu.make_async_copy(rows_ref.at[0], new_ref.at[:, 0:16, :], sems.at[0]),
        pltpu.make_async_copy(rows_ref.at[1], new_ref.at[:, 240:256, :], sems.at[1]),
    ]
    for copy in copies:
        copy.start()
    for copy in copies:
        copy.wait()


def patch(columns, part, top, bottom, above, below, total, more):
    anywhere = pl.BlockSpec(memory_space=pltpu.HBM)
    return pl.pallas_call(
        functools.partial(patch_body, columns),
        out_shape=jax.ShapeDtypeStruct((NV, 256, LEV), F32),
        in_specs=[anywhere] + [vmem()] * 6,
        out_specs=anywhere,
        scratch_shapes=[pltpu.VMEM((2, NV, N, LEV), F32), pltpu.SemaphoreType.DMA((2,))],
        input_output_aliases={0: 0},
        compiler_params=pltpu.CompilerParams(vmem_limit_bytes=6 << 20),
        cost_estimate=pl.CostEstimate(flops=10**6, bytes_accessed=10**6, transcendentals=0),
        name="patch",
    )(part, top, bottom, above, below, total, more)


def shifted(value, axis, by):
    count = lax.axis_size(axis)
    return lax.ppermute(value, axis, [(i, (i + by) % count) for i in range(count)])


def partner(value, axis, bit):
    count = lax.axis_size(axis)
    return lax.ppermute(value, axis, [(i, i ^ bit) for i in range(count)])


def exchanged(low, high, axis):
    from_low = shifted(high, axis, 1)
    return from_low, shifted(low, axis, -1)


def per_device(state, wind_x, wind_y, level_mix, field_mix, block_cost):
    state = state.reshape(NV, 256, LEV)
    wind_x = wind_x.reshape(256, LEV)
    wind_y = wind_y.reshape(256, LEV)
    slab = (256, LEV)
    edge12, edge13 = (NV, N, LEV), (NF, N, LEV)
    state, wxs, wys, edge, left, right = call(
        first_body,
        tuple(pltpu.with_memory_space_constraint(x, pltpu.HBM) for x in (state, wind_x, wind_y)),
        ((NV, 256, LEV), slab, slab, (2, 5, N, LEV), edge12, edge12), 1, hbm=3,
        scratch=(
            pltpu.VMEM(slab, BF16), pltpu.VMEM(slab, BF16), pltpu.SemaphoreType.DMA((NV + 2,)),
        ),
    )
    from_left, from_right = exchanged(left, right, "narrow")
    (g,) = call(functools.partial(full_body, NV), (state, wxs, wys), ((NV, 256, LEV),), 3)
    top, bottom, moved = call(
        start_body, (state, g, from_left, from_right),
        (edge12, edge12, (NV, 256, LEV)), 0.6,
    )
    above, below = exchanged(top, bottom, "wide")
    raw, total, s = call(
        physics_body, (block_cost, state, level_mix, field_mix, moved),
        ((NV, 256, LEV), (NV, LEV), (NF, 256, LEV)), 20,
        scratch=(pltpu.VMEM((96, 256), BF16), pltpu.VMEM((256, 256), BF16)), smem=1,
    )
    more = partner(total, "wide", 8)
    plan = [
        [("wide", 4)], [("narrow", 1), ("narrow", 2), ("narrow", 3)],
        [("wide", 2)], [("wide", 1)], [("narrow", 4)],
    ]
    window = 0

    def next_sum(passed, more):
        nonlocal window
        total = passed + more
        if window < len(plan):
            parts = []
            for step in plan[window]:
                parts.append(partner(total, *step))
            more = functools.reduce(jnp.add, parts)
        window += 1
        return total, more

    columns = 256 * lax.axis_size("wide") * lax.axis_size("narrow")
    for k in range(1, NSUB):
        s, left, right = call(
            edges_body, (s, above, below, edge),
            ((NF, 256, LEV), edge13, edge13), 0.7,
        )
        from_left, from_right = exchanged(left, right, "narrow")
        g, total = call(
            functools.partial(full_body, NF), (s, wxs, wys, total),
            ((NF, 256, LEV), (NV, LEV)), 3,
        )
        total, more = next_sum(total, more)
        top, bottom = call(
            functools.partial(rows_body, NF), (g, from_left, from_right),
            (edge13, edge13), 0.3,
        )
        above, below = exchanged(top, bottom, "wide")
        if k < NSUB - 1:
            s, total = call(
                update_body, (s, g, from_left, from_right, raw, total),
                ((NF, 256, LEV), (NV, LEV)), 1,
            )
            total, more = next_sum(total, more)
    part, tendency, top, bottom = output(
        columns, s, g, from_left, from_right, raw, total, more
    )
    new_state = patch(columns, part, top, bottom, above, below, total, more)
    return new_state.reshape(NV, N, N, LEV), tendency.reshape(NV, N, N, LEV)


def solution(mesh):
    placed = (
        P(None, "wide", "narrow", None),
        P("wide", "narrow", None),
        P("wide", "narrow", None),
        P(),
        P(),
        P("wide", "narrow"),
    )
    return jax.shard_map(
        per_device,
        mesh=mesh,
        in_specs=placed,
        out_specs=(P(None, "wide", "narrow", None), P(None, "wide", "narrow", None)),
        check_vma=False,
    )
```

```python
import functools
import math

import jax
import jax.numpy as jnp
import numpy as np
from jax import lax
from jax.experimental import pallas as pl
from jax.experimental.pallas import tpu as pltpu
from jax.sharding import PartitionSpec as P


NV = 12
NF = NV + 1
LEV = 128
N = 16
NSUB = 4
STEP = 0.05
F32 = jnp.float32
BF16 = jnp.bfloat16
EXTRA = 8


def derivative_numbers():
    nodes = np.array([-1.0, -1.0 / math.sqrt(5.0), 1.0 / math.sqrt(5.0), 1.0])
    spacing = nodes[:, None] - nodes[None, :] + np.eye(4)
    weights = 1.0 / np.prod(spacing, axis=1)
    off = weights[None, :] / weights[:, None] / spacing * (1.0 - np.eye(4))
    return off - np.diag(off.sum(1))


DER = derivative_numbers()
COPIES = np.array([2.0, 1.0, 1.0, 2.0])
DERC = DER / COPIES[:, None]


def vmem():
    return pl.BlockSpec(memory_space=pltpu.VMEM)


def call(body, ins, outs, micros, aliases=None, scratch=(), smem=0, hbm=0):
    specs = [pl.BlockSpec(memory_space=pltpu.SMEM)] * smem
    specs += [pl.BlockSpec(memory_space=pltpu.HBM)] * hbm
    specs += [vmem()] * (len(ins) - smem - hbm)
    return pl.pallas_call(
      body,
      out_shape=tuple(
          o if isinstance(o, jax.ShapeDtypeStruct) else jax.ShapeDtypeStruct(o, F32) for o in outs
      ),
      in_specs=specs,
      out_specs=tuple(vmem() for _ in outs),
      scratch_shapes=list(scratch),
      input_output_aliases=aliases or {},
      compiler_params=pltpu.CompilerParams(vmem_limit_bytes=6 << 20),
      cost_estimate=pl.CostEstimate(
          flops=int(micros * 4e6), bytes_accessed=int(micros * 2e6), transcendentals=0
      ),
    )(*ins)


def field_operator(field_mix):
    row = lax.broadcasted_iota(jnp.int32, (96, NV), 0) // 8
    pick = (row == lax.broadcasted_iota(jnp.int32, (96, NV), 1)).astype(F32)
    wide = lax.dot_general(
        pick, field_mix, (((1,), (0,)), ((), ())),
        precision=lax.Precision.HIGHEST, preferred_element_type=F32,
    )
    wide = lax.dot_general(
        wide, pick, (((1,), (1,)), ((), ())),
        precision=lax.Precision.HIGHEST, preferred_element_type=F32,
    )
    left = lax.broadcasted_iota(jnp.int32, (96, 96), 0) % 8
    right = lax.broadcasted_iota(jnp.int32, (96, 96), 1) % 8
    wide = jnp.where(left == right, wide, 0.0)
    high = wide.astype(BF16)
    low = (wide - high.astype(F32)).astype(BF16)
    return high, low


PARTS = 2


def field_weights(level_ref, mix_ref, field_w, level_w):
    high, low = field_operator(mix_ref[...])
    field_w[:, :96] = high
    field_w[:, 96:192] = low
    field_w[:, 192:] = high[:, : 8 * EXTRA]
    level_w[...] = jnp.zeros_like(level_w)
    level_w[:LEV, :LEV] = level_ref[...]
    level_w[LEV:, LEV:] = level_ref[...]


def turns(x_ref, field_w, level_w, rows):
    def part(row, half):
        return (slice(None), slice(16 * row + 8 * half, 16 * row + 8 * half + 8), slice(None))

    now = [[x_ref[part(r, h)].reshape(96, LEV) for h in range(2)] for r in rows]
    packed = [jnp.concatenate([x.astype(BF16) for x in pair], axis=1) for pair in now]
    mixed = jnp.dot(jnp.concatenate(packed, axis=0), level_w[...], preferred_element_type=F32)
    for i, r in enumerate(rows):
        y = mixed[96 * i : 96 * i + 96]
        y_high = y.astype(BF16)
        y_low = (y[: 8 * EXTRA] - y_high[: 8 * EXTRA].astype(F32)).astype(BF16)
        coupled = jnp.dot(
            field_w[...],
            jnp.concatenate([y_high, y_high, y_low], axis=0),
            preferred_element_type=F32,
        )
        for h in range(2):
            value = jnp.tanh(coupled[:, LEV * h : LEV * h + LEV])
            x_ref[part(r, h)] = (0.5 * (now[i][h] + value)).reshape(NV, 8, LEV)


def joint_turns(index, count_ref, x_ref, field_w, level_w):
    both = jnp.minimum(count_ref[0, 0], count_ref[1, 0])

    def joint(i, carry):
        turns(x_ref, field_w, level_w, range(16))
        return carry

    lax.fori_loop(both * index // PARTS, both * (index + 1) // PARTS, joint, 0)
    return both


def physics_first(count_ref, state_ref, level_ref, mix_ref, x_ref, field_w, level_w):
    field_weights(level_ref, mix_ref, field_w, level_w)
    x_ref[...] = state_ref[...]
    joint_turns(0, count_ref, x_ref, field_w, level_w)


def physics_last(
    count_ref, before_ref, field_w, level_w, state_ref, moved_ref, raw_ref, sum_ref, s_ref
):
    raw_ref[...] = before_ref[...]
    both = joint_turns(PARTS - 1, count_ref, raw_ref, field_w, level_w)
    for block in range(2):

        def single(i, carry, block=block):
            turns(raw_ref, field_w, level_w, range(8 * block, 8 * block + 8))
            return carry

        lax.fori_loop(both, count_ref[block, 0], single, 0)

    def finish(v, carry):
        raw = raw_ref[v] - state_ref[v]
        raw_ref[v] = raw
        s_ref[v] = moved_ref[v] + STEP * raw
        sum_ref[pl.ds(v, 1), :] = jnp.sum(raw, axis=0, keepdims=True)
        return carry

    lax.fori_loop(0, NV, finish, 0, unroll=2)
    s_ref[NV] = jnp.full((256, LEV), STEP, F32)


def column_table(shift):
    b = lax.broadcasted_iota(jnp.int32, (8, LEV), 0) % 4
    out = jnp.full((8, LEV), float(DERC[3, 3 ^ shift]), F32)
    for k in range(3):
        out = jnp.where(b == k, float(DERC[k, k ^ shift]), out)
    return out


def tables():
    return [column_table(s) for s in range(4)]


def permuted(x, index):
    return jnp.take_along_axis(x, index, axis=0)


def indices():
    q = lax.broadcasted_iota(jnp.int32, (8, LEV), 0)
    return [q ^ s for s in range(4)]


def along_sublanes(x, coef, index):
    out = coef[0] * x
    for s in range(1, 4):
        out = out + coef[s] * permuted(x, index[s])
    return out


def column_edges(s_ref, v, edge_ref, side, half, coef, index):
    q0 = 0 if side == 0 else 12
    edge = 0 if side == 0 else 3
    rows = []
    for j in range(4):
        rows.append(s_ref[v, pl.ds(128 * half + q0 + j, 8, stride=16), :])
    out = along_sublanes(edge_ref[side, 4, pl.ds(8 * half, 8), :] * rows[edge], coef, index)
    for j in range(4):
        out = out + edge_ref[side, j, pl.ds(8 * half, 8), :] * rows[j]
    return out


def write_edges(fields, s_ref, edge_ref, left_ref, right_ref):
    coef, index = tables(), indices()

    def one(v, carry):
        for side, ref in ((0, left_ref), (1, right_ref)):
            for half in range(2):
                ref[v, pl.ds(8 * half, 8), :] = column_edges(
                    s_ref, v, edge_ref, side, half, coef, index
                )
        return carry

    lax.fori_loop(0, fields, one, 0)


def first_body(
    state_hbm, wx_hbm, wy_hbm, s_ref, wxs_ref, wys_ref, edge_ref, left_ref, right_ref,
    wx_ref, wy_ref, sems,
):
    winds = [
        pltpu.make_async_copy(wx_hbm, wx_ref, sems.at[NV]),
        pltpu.make_async_copy(wy_hbm, wy_ref, sems.at[NV + 1]),
    ]
    fields = [
        pltpu.make_async_copy(state_hbm.at[v], s_ref.at[v], sems.at[v]) for v in range(NV)
    ]
    for copy in winds + fields:
        copy.start()
    for copy in winds:
        copy.wait()
    q = lax.broadcasted_iota(jnp.int32, (16, LEV), 0) % 4
    inner = (q == 1) | (q == 2)
    per_q = jnp.where(inner, -STEP, -0.5 * STEP)
    for p in range(N):
        rows = pl.ds(16 * p, 16)
        wxs_ref[rows, :] = per_q * wx_ref[rows, :].astype(F32)
        wys_ref[rows, :] = float(-STEP / COPIES[p % 4]) * wy_ref[rows, :].astype(F32)
    for side in range(2):
        q0, edge = (0, 0) if side == 0 else (12, 3)
        for half in range(2):
            at = pl.ds(8 * half, 8)
            for j in range(4):
                wind = wys_ref[pl.ds(128 * half + q0 + j, 8, stride=16), :]
                edge_ref[side, j, at, :] = float(DERC[edge, j]) * wind
            edge_ref[side, 4, at, :] = wxs_ref[pl.ds(128 * half + q0 + edge, 8, stride=16), :]
    for copy in fields:
        copy.wait()
    write_edges(NV, s_ref, edge_ref, left_ref, right_ref)


def along_rows(f):
    c = DERC
    plus, minus = f[0] + f[3], f[0] - f[3]
    inner_plus, inner_minus = f[1] + f[2], f[1] - f[2]
    even = plus - inner_plus
    a = float(0.5 * (c[0, 0] - c[0, 3])) * minus + float(0.5 * (c[0, 1] - c[0, 2])) * inner_minus
    b = float(0.5 * (c[0, 0] + c[0, 3])) * even
    d = float(0.5 * (c[1, 0] - c[1, 3])) * minus + float(0.5 * (c[1, 1] - c[1, 2])) * inner_minus
    e = float(0.5 * (c[1, 0] + c[1, 3])) * even
    return [a + b, d + e, d - e, a - b]


def full_body(fields, s_ref, wxs_ref, wys_ref, *refs):
    if len(refs) == 3:
        refs[2][...] = refs[0][...]
    g_ref = refs[len(refs) // 2]
    coef, index = tables(), indices()
    q = lax.broadcasted_iota(jnp.int32, (8, LEV), 0)
    middle = (q == 3) | (q == 4)
    low, high = q == 0, q == 7
    swap = jnp.where(low, 7, jnp.where(high, 0, jnp.where(middle, 7 - q, q)))

    def one(v, carry):
        for e in range(4):
            halves = []
            for half in range(2):
                at = [pl.ds(64 * e + 16 * a + 8 * half, 8) for a in range(4)]
                s = [s_ref[v, at[a], :] for a in range(4)]
                x = along_rows([wxs_ref[at[a], :] * s[a] for a in range(4)])
                halves.append(
                    [
                        x[a] + along_sublanes(wys_ref[at[a], :] * s[a], coef, index)
                        for a in range(4)
                    ]
                )
            for a in range(4):
                left, right = halves[0][a], halves[1][a]
                p_left, p_right = permuted(left, swap), permuted(right, swap)
                left = left + jnp.where(high, p_right, jnp.where(middle, p_left, 0.0))
                right = right + jnp.where(low, p_left, jnp.where(middle, p_right, 0.0))
                g_ref[v, pl.ds(64 * e + 16 * a, 8), :] = left
                g_ref[v, pl.ds(64 * e + 16 * a + 8, 8), :] = right
        return carry

    lax.fori_loop(0, fields, one, 0)


def with_columns(g_ref, from_left, from_right, v, p, low, high):
    left = g_ref[v, pl.ds(16 * p, 8), :]
    right = g_ref[v, pl.ds(16 * p + 8, 8), :]
    left = left + jnp.where(low, from_left[v, pl.ds(p, 1), :], 0.0)
    right = right + jnp.where(high, from_right[v, pl.ds(p, 1), :], 0.0)
    return left, right


def ends():
    q = lax.broadcasted_iota(jnp.int32, (8, LEV), 0)
    return q == 0, q == 7


def rows_body(fields, g_ref, from_left, from_right, top_ref, bottom_ref):
    low, high = ends()

    def one(v, carry):
        for p, ref in ((0, top_ref), (N - 1, bottom_ref)):
            left, right = with_columns(g_ref, from_left, from_right, v, p, low, high)
            ref[v, 0:8, :] = left
            ref[v, 8:16, :] = right
        return carry

    lax.fori_loop(0, fields, one, 0)


def advance(s_ref, g_ref, from_left, from_right, v, low, high, source, out_ref, inner=False):
    g = [with_columns(g_ref, from_left, from_right, v, p, low, high) for p in range(N)]
    for p in range(N):
        mate = p + 1 if p % 4 == 3 else p - 1 if p % 4 == 0 else -1
        for half in range(2):
            at = pl.ds(16 * p + 8 * half, 8)
            value = g[p][half]
            if 0 <= mate < N:
                value = value + g[mate][half]
            value = s_ref[v, at, :] + value
            if source is not None:
                value = value + source(at)
            if inner:
                out_ref[at, :] = value
            else:
                out_ref[v, at, :] = value


def start_body(s_ref, g_ref, from_left, from_right, top_ref, bottom_ref, out_ref):
    rows_body(NV, g_ref, from_left, from_right, top_ref, bottom_ref)
    low, high = ends()

    def one(v, carry):
        advance(s_ref, g_ref, from_left, from_right, v, low, high, None, out_ref)
        return carry

    lax.fori_loop(0, NV, one, 0)


def update_body(
    s_ref, g_ref, from_left, from_right, raw_ref, sum_ref, out_ref, pass_ref
):
    pass_ref[...] = sum_ref[...]
    low, high = ends()

    def one(v, carry):
        advance(
            s_ref, g_ref, from_left, from_right, v, low, high,
            lambda at: STEP * raw_ref[v, at, :], out_ref,
        )
        return carry

    lax.fori_loop(0, NV, one, 0)
    advance(s_ref, g_ref, from_left, from_right, NV, low, high, lambda at: STEP, out_ref)


def edges_body(s_ref, above_ref, below_ref, edge_ref, out_ref, left_ref, right_ref):
    def one(v, carry):
        out_ref[v, 0:16, :] = s_ref[v, 0:16, :] + above_ref[v]
        out_ref[v, 16:240, :] = s_ref[v, 16:240, :]
        out_ref[v, 240:256, :] = s_ref[v, 240:256, :] + below_ref[v]
        return carry

    lax.fori_loop(0, NV, one, 0)
    if above_ref.shape[0] == NF:
        one(NV, 0)
    else:
        out_ref[NV] = s_ref[NV]
    write_edges(NF, out_ref, edge_ref, left_ref, right_ref)


def output_body(
    columns, s_ref, g_ref, from_left, from_right, raw_ref, sum_ref, more_ref,
    new_hbm, tend_hbm, top_ref, bottom_ref, new_ref, tend_ref, response, sems,
):
    low, high = ends()
    copies = []
    for v in range(NV):
        copies.append(pltpu.make_async_copy(tend_ref.at[v], tend_hbm.at[v], sems.at[0, v]))
        copies.append(pltpu.make_async_copy(new_ref.at[v], new_hbm.at[v], sems.at[1, v]))
    advance(s_ref, g_ref, from_left, from_right, NV, low, high, lambda at: STEP, response, True)
    for v in range(NV):
        mean = (sum_ref[v : v + 1, :] + more_ref[v : v + 1, :]) * (1.0 / columns)
        tend_ref[v] = raw_ref[v] - mean
        copies[2 * v].start()
    for v in range(NV):
        mean = (sum_ref[v : v + 1, :] + more_ref[v : v + 1, :]) * (1.0 / columns)
        advance(
            s_ref, g_ref, from_left, from_right, v, low, high,
            lambda at: STEP * raw_ref[v, at, :] - mean * response[at, :], new_ref.at[v], True,
        )
        copies[2 * v + 1].start()
        top_ref[v] = new_ref[v, 0:16, :]
        bottom_ref[v] = new_ref[v, 240:256, :]
    for copy in copies:
        copy.wait()


def output(columns, s, g, from_left, from_right, raw, total, more):
    anywhere = pl.BlockSpec(memory_space=pltpu.HBM)
    return pl.pallas_call(
      functools.partial(output_body, columns),
      out_shape=(jax.ShapeDtypeStruct((NV, 256, LEV), F32),) * 2
      + (jax.ShapeDtypeStruct((NV, N, LEV), F32),) * 2,
      in_specs=[vmem()] * 7,
      out_specs=(anywhere, anywhere, vmem(), vmem()),
      scratch_shapes=[
          pltpu.VMEM((NV, 256, LEV), F32), pltpu.VMEM((NV, 256, LEV), F32),
          pltpu.VMEM((256, LEV), F32), pltpu.SemaphoreType.DMA((2, NV)),
      ],
      compiler_params=pltpu.CompilerParams(vmem_limit_bytes=8 << 20),
      cost_estimate=pl.CostEstimate(flops=10**7, bytes_accessed=8 * 10**6, transcendentals=0),
      name="output",
    )(s, g, from_left, from_right, raw, total, more)


def patch_body(
    columns, part_ref, top_ref, bottom_ref, above_ref, below_ref, sum_ref, more_ref,
    new_ref, rows_ref, sems,
):
    for v in range(NV):
        mean = (sum_ref[pl.ds(v, 1), :] + more_ref[pl.ds(v, 1), :]) * (1.0 / columns)
        rows_ref[0, v] = top_ref[v] + above_ref[v] - mean * above_ref[NV]
        rows_ref[1, v] = bottom_ref[v] + below_ref[v] - mean * below_ref[NV]
    copies = [
        pltpu.make_async_copy(rows_ref.at[0], new_ref.at[:, 0:16, :], sems.at[0]),
        pltpu.make_async_copy(rows_ref.at[1], new_ref.at[:, 240:256, :], sems.at[1]),
    ]
    for copy in copies:
        copy.start()
    for copy in copies:
        copy.wait()


def patch(columns, part, top, bottom, above, below, total, more):
    anywhere = pl.BlockSpec(memory_space=pltpu.HBM)
    return pl.pallas_call(
        functools.partial(patch_body, columns),
        out_shape=jax.ShapeDtypeStruct((NV, 256, LEV), F32),
        in_specs=[anywhere] + [vmem()] * 6,
        out_specs=anywhere,
        scratch_shapes=[pltpu.VMEM((2, NV, N, LEV), F32), pltpu.SemaphoreType.DMA((2,))],
        input_output_aliases={0: 0},
        compiler_params=pltpu.CompilerParams(vmem_limit_bytes=6 << 20),
        cost_estimate=pl.CostEstimate(flops=10**6, bytes_accessed=10**6, transcendentals=0),
        name="patch",
    )(part, top, bottom, above, below, total, more)


def shifted(value, axis, by):
    count = lax.axis_size(axis)
    return lax.ppermute(value, axis, [(i, (i + by) % count) for i in range(count)])


def partner(value, axis, bit):
    count = lax.axis_size(axis)
    return lax.ppermute(value, axis, [(i, i ^ bit) for i in range(count)])


def exchanged(low, high, axis):
    from_low = shifted(high, axis, 1)
    return from_low, shifted(low, axis, -1)


def per_device(state, wind_x, wind_y, level_mix, field_mix, block_cost):
    state = state.reshape(NV, 256, LEV)
    wind_x = wind_x.reshape(256, LEV)
    wind_y = wind_y.reshape(256, LEV)
    slab = (256, LEV)
    edge12, edge13 = (NV, N, LEV), (NF, N, LEV)
    state, wxs, wys, edge, left, right = call(
        first_body,
        tuple(pltpu.with_memory_space_constraint(x, pltpu.HBM) for x in (state, wind_x, wind_y)),
        ((NV, 256, LEV), slab, slab, (2, 5, N, LEV), edge12, edge12), 1, hbm=3,
        scratch=(
            pltpu.VMEM(slab, BF16), pltpu.VMEM(slab, BF16), pltpu.SemaphoreType.DMA((NV + 2,)),
        ),
    )
    whole = (NV, 256, LEV)
    from_left, from_right = exchanged(left, right, "narrow")
    (g,) = call(functools.partial(full_body, NV), (state, wxs, wys), (whole,), 3)
    top, bottom, moved = call(
        start_body, (state, g, from_left, from_right), (edge12, edge12, whole), 0.6
    )
    above, below = exchanged(top, bottom, "wide")
    x, field_w, level_w = call(
        physics_first, (block_cost, state, level_mix, field_mix),
        (
            whole,
            jax.ShapeDtypeStruct((96, 256), BF16),
            jax.ShapeDtypeStruct((256, 256), BF16),
        ), 8, smem=1,
    )
    raw, total, s = call(
        physics_last, (block_cost, x, field_w, level_w, state, moved),
        (whole, (NV, LEV), (NF, 256, LEV)), 8, smem=1,
    )
    more = partner(total, "wide", 8)
    plan = [
        [("wide", 4)], [("narrow", 1), ("narrow", 2), ("narrow", 3)],
        [("wide", 2)], [("wide", 1)], [("narrow", 4)],
    ]
    window = 0

    def next_sum(passed, more):
        nonlocal window
        total = passed + more
        if window < len(plan):
            parts = []
            for step in plan[window]:
                parts.append(partner(total, *step))
            more = functools.reduce(jnp.add, parts)
        window += 1
        return total, more

    columns = 256 * lax.axis_size("wide") * lax.axis_size("narrow")
    for k in range(1, NSUB):
        s, left, right = call(
            edges_body, (s, above, below, edge),
            ((NF, 256, LEV), edge13, edge13), 0.7,
        )
        from_left, from_right = exchanged(left, right, "narrow")
        g, total = call(
            functools.partial(full_body, NF), (s, wxs, wys, total),
            ((NF, 256, LEV), (NV, LEV)), 3,
        )
        total, more = next_sum(total, more)
        top, bottom = call(
            functools.partial(rows_body, NF), (g, from_left, from_right),
            (edge13, edge13), 0.3,
        )
        above, below = exchanged(top, bottom, "wide")
        if k < NSUB - 1:
            s, total = call(
                update_body, (s, g, from_left, from_right, raw, total),
                ((NF, 256, LEV), (NV, LEV)), 1,
            )
            total, more = next_sum(total, more)
    part, tendency, top, bottom = output(
        columns, s, g, from_left, from_right, raw, total, more
    )
    new_state = patch(columns, part, top, bottom, above, below, total, more)
    return new_state.reshape(NV, N, N, LEV), tendency.reshape(NV, N, N, LEV)


def solution(mesh):
    placed = (
        P(None, "wide", "narrow", None),
        P("wide", "narrow", None),
        P("wide", "narrow", None),
        P(),
        P(),
        P("wide", "narrow"),
    )
    return jax.shard_map(
        per_device,
        mesh=mesh,
        in_specs=placed,
        out_specs=(P(None, "wide", "narrow", None), P(None, "wide", "narrow", None)),
        check_vma=False,
    )
```
